32 devices in a mesh: grp: 2 (over x), sp: 16 (over z, y, core).
Axes of the slice: x: 2, y: 2, z: 4, core: 2. Of those that a mesh axis runs over, the one named last changes fastest.
Arguments:
- field_in: bfloat16 [256, 16, 128, 512], P(('grp', 'sp')), parts along dimension 0, may hold values from -6 to 6
- out_grad: bfloat16 [256, 16, 128, 512], P(('grp', 'sp')), parts along dimension 0, may hold values from -6 to 6
- spectral_weight: bfloat16 [192, 96, 2, 256], P('sp'), may hold values from -6 to 6
- bypass_weight: bfloat16 [16, 16], replicated, may hold values from -1.5 to 1.5
- mode_x: int32 [12], replicated, may hold values from 0 to 127, as said below
- mode_y: int32 [16], replicated, may hold values from 0 to 127, as said below
- mode_z: int32 [12], replicated, may hold values from 0 to 31, as said below
- mode_t: int32 [8], replicated, may hold values from 0 to 15, as said below
Outputs:
- in_grad: bfloat16 [256, 16, 128, 512], P(('grp', 'sp')), parts along dimension 0
- weight_grad: float32 [384, 96, 2, 256], P(('grp', 'sp')), parts along dimension 0
- bypass_grad: float32 [32, 16], P('grp'), parts along dimension 0
The draws below stay inside these ranges and needn't reach their ends.
There are 2 independent parts, one for each index of `grp`. The reference program is written for one: setup_inputs(seed, part) draws one part's arguments, and reference() takes and returns one part's arrays. A program takes and returns all parts, laid end to end along the dimension named above; an argument that names none is the same for every part. Nothing has to cross between parts.
Inputs may be any that keep to these rules, and one draw needn't show every extreme that they name: `mode_x`: 12 distinct frequencies, among them 0 and 127. `mode_y`: 16 distinct frequencies, among them 0 and 127. `mode_z`: 12 distinct frequencies, among them 0 and 31. `mode_t`: 8 distinct frequencies, among them 0 and 15.
All inputs are finite; a program needn't handle non-finite values.
Results may differ from the reference program's by a relative error of at most 0.0015.
Values sent between devices are 32-bit elements; how exact they have to be, the bound alone decides.
No kernel may reach another device: no remote copies, remote signals or barrier semaphores. Data moves between devices by JAX's collectives and lax.ppermute only.
A program may use at most 192 MiB of HBM per device.

```python
import math
import jax
import jax.numpy as jnp
from jax import lax

X = 128
Y = 128
Z = 32
STEPS = 16
C = 16
KX = 12
KY = 16
KZ = 12
KT = 8


def pick_modes(seed_key, amount, length):
    key_rest, key_order = jax.random.split(seed_key)
    interior = jax.random.permutation(key_rest, length - 2)[:amount - 2] + 1
    corners = jnp.array([0, length - 1], dtype=jnp.int32)
    chosen = jnp.concatenate([corners, interior.astype(jnp.int32)])
    return jax.random.permutation(key_order, chosen)


def draw_mode_x(key, part):
    return pick_modes(jax.random.fold_in(key, 11), KX, X)


def draw_mode_y(key, part):
    return pick_modes(jax.random.fold_in(key, 23), KY, Y)


def draw_mode_z(key, part):
    return pick_modes(jax.random.fold_in(key, 37), KZ, Z)


def draw_mode_t(key, part):
    return pick_modes(jax.random.fold_in(key, 41), KT, STEPS)


def block_scale(key, dims, cuts, smallest, largest):
    def one(dim, parts):
        steps = jax.random.uniform(jax.random.fold_in(jax.random.fold_in(key, 6), dim), (parts,), jnp.float32, smallest / len(cuts), largest / len(cuts))
        return jnp.repeat(jnp.exp(steps), dims[dim] // parts).reshape((-1,) + (1,) * (len(dims) - dim - 1))

    loudness = one(*cuts[0])
    for cut in cuts[1:]:
        loudness = loudness * one(*cut)
    return loudness


def scatter_about(key, shape, scale, limit, cuts=(), held_as=jnp.bfloat16):
    drawn = scale * jax.random.normal(key, shape, jnp.float32)
    if cuts:
        drawn = drawn * block_scale(key, shape, cuts, -0.22, 0.18)
    return jnp.clip(drawn, -limit, limit).astype(held_as)


def setup_inputs(seed: int = 0, part: int = 0) -> dict:
    key_list = jax.random.split(jax.random.key(seed), 9)
    own_keys = jax.random.split(jax.random.fold_in(key_list[8], part), 9)
    field_in = scatter_about(own_keys[0], (X, C, Y, Z * STEPS), 1.0, 6.0, ((0, 16),))
    out_grad = scatter_about(own_keys[1], (X, C, Y, Z * STEPS), 1.0, 6.0, ((0, 16),))
    spectral_weight = scatter_about(key_list[2], (KY * KZ, KX * KT, 2, C * C), 1.5, 6.0, ((0, 16),))
    bypass_weight = scatter_about(key_list[3], (C, C), C ** -0.5, 1.5)
    mode_x = draw_mode_x(jax.random.fold_in(key_list[8], 71), part)
    mode_y = draw_mode_y(jax.random.fold_in(key_list[8], 71), part)
    mode_z = draw_mode_z(jax.random.fold_in(key_list[8], 71), part)
    mode_t = draw_mode_t(jax.random.fold_in(key_list[8], 71), part)
    return {"field_in": field_in, "out_grad": out_grad, "spectral_weight": spectral_weight, "bypass_weight": bypass_weight, "mode_x": mode_x, "mode_y": mode_y, "mode_z": mode_z, "mode_t": mode_t}


HIGH = lax.Precision.HIGHEST

def block_table(frequencies, length):
    positions = jnp.arange(length, dtype=jnp.int32)
    phase_ints = positions[:, None] * frequencies[None, :].astype(jnp.int32) % length
    angles = 2.0 * math.pi / length * phase_ints.astype(jnp.float32)
    factor = 1.0 / math.sqrt(length)
    cosines = jnp.cos(angles) * factor
    sines = jnp.sin(angles) * factor
    real_in = jnp.stack([cosines, -sines], axis=-1)
    imag_in = jnp.stack([sines, cosines], axis=-1)
    return jnp.stack([real_in, imag_in], axis=1)

def plane_table(modes_depth, modes_time):
    depth_pos = jnp.arange(Z, dtype=jnp.int32)
    step_pos = jnp.arange(STEPS, dtype=jnp.int32)
    part_z = depth_pos[:, None] * modes_depth[None, :].astype(jnp.int32) % Z
    part_t = step_pos[:, None] * modes_time[None, :].astype(jnp.int32) % STEPS
    phase_ints = (part_z[:, None, :, None] * STEPS + part_t[None, :, None, :] * Z) % (Z * STEPS)
    angles = 2.0 * math.pi / (Z * STEPS) * phase_ints.astype(jnp.float32)
    factor = 1.0 / math.sqrt(Z * STEPS)
    table = jnp.stack([jnp.cos(angles), -jnp.sin(angles)], axis=2) * factor
    return table.reshape(Z * STEPS, 2 * KZ * KT)

def mixing(spec_u, spec_g, weights):
    modes_dev = spec_u.shape[0]
    wfull = weights.astype(jnp.float32).reshape(modes_dev, KX, KT, 2, C, C)
    w_re = wfull[:, :, :, 0]
    w_im = wfull[:, :, :, 1]
    u_re = spec_u[:, :, :, 0]
    u_im = spec_u[:, :, :, 1]
    g_re = spec_g[:, :, :, 0]
    g_im = spec_g[:, :, :, 1]
    adj_re = jnp.einsum('mktco,mkto->mktc', w_re, g_re, precision=HIGH) + jnp.einsum('mktco,mkto->mktc', w_im, g_im, precision=HIGH)
    adj_im = jnp.einsum('mktco,mkto->mktc', w_re, g_im, precision=HIGH) - jnp.einsum('mktco,mkto->mktc', w_im, g_re, precision=HIGH)
    grad_re = u_re[..., :, None] * g_re[..., None, :] + u_im[..., :, None] * g_im[..., None, :]
    grad_im = u_re[..., :, None] * g_im[..., None, :] - u_im[..., :, None] * g_re[..., None, :]
    adjoint = jnp.stack([adj_re, adj_im], axis=3)
    gradient = jnp.stack([grad_re, grad_im], axis=3).reshape(modes_dev, KX * KT, 2, C * C)
    return (adjoint, gradient)

def forward_spectra(field, plane, ytab, xtab):
    planes_zt = jnp.einsum('xcyn,nm->xcym', field.astype(jnp.float32), plane, precision=HIGH)
    planes_zt = planes_zt.reshape(X, C, Y, 2, KZ, KT)
    spectra = jnp.einsum('xcypzt,ypkq->xkzcqt', planes_zt, ytab, precision=HIGH)
    spectra = spectra.reshape(X, KY * KZ, C, 2, KT)
    return jnp.einsum('xmcpt,xpkq->mktqc', spectra, xtab, precision=HIGH)

def reference(field_in, out_grad, spectral_weight, bypass_weight, mode_x, mode_y, mode_z, mode_t):
    plane = plane_table(mode_z, mode_t)
    ytab = block_table(mode_y, Y)
    xtab = block_table(mode_x, X)
    spec_u = forward_spectra(field_in, plane, ytab, xtab)
    spec_g = forward_spectra(out_grad, plane, ytab, xtab)
    adjoint, weight_grad = mixing(spec_u, spec_g, spectral_weight)
    slabs = jnp.einsum('mktpc,xqkp->xmcqt', adjoint, xtab, precision=HIGH)
    slabs = slabs.reshape(X, KY, KZ, C, 2, KT)
    planes_zt = jnp.einsum('xkzcpt,yqkp->xcyqzt', slabs, ytab, precision=HIGH).reshape(X, C, Y, 2 * KZ * KT)
    spectral = jnp.einsum('xcym,nm->xcyn', planes_zt, plane, precision=HIGH)
    bypass = jnp.einsum('co,xoyn->xcyn', bypass_weight.astype(jnp.float32), out_grad.astype(jnp.float32), precision=HIGH)
    in_grad = (spectral + bypass).astype(jnp.bfloat16)
    total = jnp.einsum('xcyn,xoyn->co', field_in.astype(jnp.float32), out_grad.astype(jnp.float32), precision=HIGH)
    bypass_grad = total / math.sqrt(X * Y * Z * STEPS)
    return (in_grad, weight_grad, bypass_grad)
```

```python
import functools
import math

import jax
import jax.numpy as jnp
from jax import lax
from jax.experimental import pallas as pl
from jax.experimental.pallas import tpu as pltpu
from jax.sharding import PartitionSpec as P

F32 = jnp.float32
BF16 = jnp.bfloat16
LANES = 128
NT = (((1,), (1,)), ((), ()))
NN = (((1,), (0,)), ((), ()))


def mm(a, b, dims=NN):
    return lax.dot_general(a, b, dims, preferred_element_type=F32)


def split(a):
    hi = a.astype(BF16)
    return hi, (a - hi.astype(F32)).astype(BF16)


def mm3(a_hi, a_lo, b_hi, b_lo, dims=NN):
    return mm(a_hi, b_hi, dims) + (mm(a_hi, b_lo, dims) + mm(a_lo, b_hi, dims))


def split_table(table):
    hi = lax.reduce_precision(table, 8, 7)
    return hi.astype(BF16), (table - hi).astype(BF16)


def params(**kw):
    return pltpu.CompilerParams(vmem_limit_bytes=48 * 1024 * 1024, **kw)


def spectra_step(field, ty, p_hi, p_lo, a_hi, a_lo, s_all, step):
    chans = field.shape[1]
    ky = ty.shape[0] // 4
    width = field.shape[3]
    for c in range(chans):
        both = mm(ty[...], field[0, c])
        part = both[: 2 * ky] + both[2 * ky :]
        hi, lo = split(part)
        rows = slice(c * ky, (c + 1) * ky)
        a_hi[rows, :width] = hi[:ky]
        a_hi[rows, width:] = hi[ky:]
        a_lo[rows, :width] = lo[:ky]
        a_lo[rows, width:] = lo[ky:]
    res = mm3(a_hi[...], a_lo[...], p_hi[...], p_lo[...])
    for p in range(2):
        s_all[step, p] = res[:, p * LANES : (p + 1) * LANES]


def spectra_end(m_hi, m_lo, out, s_all, ky, used):
    slabs, _, rows, _ = s_all.shape
    chans = rows // ky

    def one(j, carry):
        pieces = [
            s_all[x, p, pl.ds(j, chans, stride=ky), :]
            for p in range(2)
            for x in range(slabs)
        ]
        s_t = jnp.concatenate(pieces, axis=0).T
        hi, lo = split(s_t)
        res = mm3(hi, lo, m_hi[...], m_lo[...])
        out[pl.ds(pl.multiple_of(j * used, 8), used), :] = res[:used]
        return carry

    lax.fori_loop(0, ky, one, 0, unroll=2)


def forward_kernel(field, ty, p_hi, p_lo, m_hi, m_lo, out, a_hi, a_lo, s_all, *, used):
    step = pl.program_id(0)
    spectra_step(field, ty, p_hi, p_lo, a_hi, a_lo, s_all, step)

    @pl.when(step == pl.num_programs(0) - 1)
    def _():
        spectra_end(m_hi, m_lo, out, s_all, ty.shape[0] // 4, used)


def forward_both_kernel(
    field, grad, ty, p_hi, p_lo, m_hi, m_lo, out, gram_out, a_hi, a_lo, s_all, gram, *, used
):
    step = pl.program_id(0)
    chans, height, width = field.shape[1:]
    blk = 16

    @pl.when(step == 0)
    def _():
        gram[...] = jnp.zeros_like(gram)

    spectra_step(field, ty, p_hi, p_lo, a_hi, a_lo, s_all, step)
    total = gram[...]
    for b in range(height // blk):
        rows = slice(b * blk, (b + 1) * blk)
        left = field[0, :, rows, :].reshape(chans * blk, width)
        right = grad[0, :, rows, :].reshape(chans * blk, width)
        total = total + mm(left, right, NT)
    gram[...] = total

    @pl.when(step == pl.num_programs(0) - 1)
    def _():
        spectra_end(m_hi, m_lo, out, s_all, ty.shape[0] // 4, used)
        gram_out[...] = gram[...]


def whole(shape):
    return pl.BlockSpec(shape, lambda *_: (0,) * len(shape), pipeline_mode=pl.Buffered(1))


def forward(fields, tabs, used):
    slabs, chans, height, width = fields[0].shape
    ty, p_hi, p_lo, m_hi, m_lo = tabs
    ky = ty.shape[0] // 4
    with_gram = len(fields) == 2
    block = pl.BlockSpec((1, chans, height, width), lambda i: (i, 0, 0, 0))
    outs = [jax.ShapeDtypeStruct((ky * used, m_hi.shape[1]), F32)]
    scratch = [
        pltpu.VMEM((chans * ky, 2 * width), BF16),
        pltpu.VMEM((chans * ky, 2 * width), BF16),
        pltpu.VMEM((slabs, 2, chans * ky, LANES), F32),
    ]
    if with_gram:
        outs.append(jax.ShapeDtypeStruct((chans * 16, chans * 16), F32))
        scratch.append(pltpu.VMEM((chans * 16, chans * 16), F32))
    kernel = forward_both_kernel if with_gram else forward_kernel
    res = pl.pallas_call(
        functools.partial(kernel, used=used),
        grid=(slabs,),
        in_specs=[block] * len(fields) + [whole(t.shape) for t in tabs],
        out_specs=[whole(o.shape) for o in outs],
        out_shape=outs,
        scratch_shapes=scratch,
        compiler_params=params(),
        name="forward_both" if with_gram else "forward_one",
        cost_estimate=pl.CostEstimate(
            flops=int(2e10), bytes_accessed=2 * sum(f.size for f in fields), transcendentals=0
        ),
    )(*fields, *tabs)
    return res if with_gram else res[0]


def mix_kernel(g, w_re, w_im, spread, gather, out):
    kx, kt = w_re.shape[1], w_re.shape[2]
    modes, chans2 = w_re.shape[0], w_re.shape[3]
    rows = modes * kt
    per = LANES // 16
    nblk = g.shape[1] // LANES
    acc = [jnp.zeros((rows, LANES), F32) for _ in range(nblk)]
    halves = []
    for b in range(nblk):
        hi, lo = split(g[:, b * LANES : (b + 1) * LANES])
        halves.append(jnp.concatenate([hi, lo], axis=1))
    for k in range(kx):
        i_re, i_im = k, kx + k
        e_re = mm(halves[i_re // per], spread[i_re % per])
        e_im = mm(halves[i_im // per], spread[i_im % per])
        wr = w_re[:, k].reshape(rows, chans2).astype(F32)
        wi = w_im[:, k].reshape(rows, chans2).astype(F32)
        for q, prod in ((i_re, wr * e_re + wi * e_im), (i_im, wr * e_im - wi * e_re)):
            hi, lo = split(prod)
            mat = gather[q % per]
            acc[q // per] = acc[q // per] + (mm(hi, mat) + mm(lo, mat))
    for b in range(nblk):
        out[:, b * LANES : (b + 1) * LANES] = acc[b]


def mix(g, w_re, w_im, spread, gather):
    return pl.pallas_call(
        mix_kernel,
        out_shape=jax.ShapeDtypeStruct(g.shape, F32),
        compiler_params=params(),
        name="mix",
        cost_estimate=pl.CostEstimate(flops=int(1e9), bytes_accessed=4 * 10**6, transcendentals=0),
    )(g, w_re, w_im, spread, gather)


def wgrad_kernel(u, g, spread_c, spread_o, out_re, out_im):
    modes, kx, kt, _ = out_re.shape
    per = LANES // 16
    nblk = g.shape[1] // LANES
    halves = []
    for ref in (u, g):
        parts = []
        for b in range(nblk):
            hi, lo = split(ref[:, b * LANES : (b + 1) * LANES])
            parts.append(jnp.concatenate([hi, lo], axis=1))
        halves.append(parts)
    for k in range(kx):
        i_re, i_im = k, kx + k
        u_re = mm(halves[0][i_re // per], spread_c[i_re % per])
        u_im = mm(halves[0][i_im // per], spread_c[i_im % per])
        g_re = mm(halves[1][i_re // per], spread_o[i_re % per])
        g_im = mm(halves[1][i_im // per], spread_o[i_im % per])
        out_re[:, k] = (u_re * g_re + u_im * g_im).reshape(modes, kt, -1)
        out_im[:, k] = (u_re * g_im - u_im * g_re).reshape(modes, kt, -1)


def wgrad(u, g, spread_c, spread_o, shape):
    return pl.pallas_call(
        wgrad_kernel,
        out_shape=[jax.ShapeDtypeStruct(shape, F32)] * 2,
        compiler_params=params(),
        name="wgrad",
        cost_estimate=pl.CostEstimate(flops=int(1e9), bytes_accessed=4 * 10**6, transcendentals=0),
    )(u, g, spread_c, spread_o)


def inverse_kernel(
    grad, adj, m_hi, m_lo, pi_hi, pi_lo, tyi, bmat, out, l_all, acc, *, used, slabs
):
    step = pl.program_id(0)
    chans, height, width = grad.shape[1:]
    ky = adj.shape[0] // used
    blk = 16

    @pl.when(step == 0)
    def _():
        def one(jj, carry):
            rows = []
            for i in range(2):
                start = pl.multiple_of((2 * jj + i) * used, 8)
                rows.append(adj[pl.ds(start, used), :])
                if used < LANES:
                    rows.append(jnp.zeros((LANES - used, adj.shape[1]), F32))
            hi, lo = split(jnp.concatenate(rows, axis=0))
            h = mm3(m_hi[...], m_lo[...], hi, lo, NT)
            for i in range(2):
                for p in range(2):
                    for x in range(slabs):
                        r = (p * slabs + x) * chans
                        l_all[x, p, pl.ds(2 * jj + i, chans, stride=ky), :] = h[
                            r : r + chans, i * LANES : (i + 1) * LANES
                        ]
            return carry

        lax.fori_loop(0, ky // 2, one, 0)

    for b in range(height // blk):
        rows = slice(b * blk, (b + 1) * blk)
        right = grad[0, :, rows, :].reshape(chans * blk, width)
        acc[:, rows, :] = mm(bmat[...], right).reshape(chans, blk, width)
    l_hi, l_lo = split(jnp.concatenate([l_all[step, 0], l_all[step, 1]], axis=1))
    h2 = mm3(l_hi, l_lo, pi_hi[...], pi_lo[...])
    for c in range(chans):
        rows = slice(c * ky, (c + 1) * ky)
        re_hi, re_lo = split(h2[rows, :width])
        im_hi, im_lo = split(h2[rows, width:])
        rhs = jnp.concatenate([re_hi, im_hi, re_lo, im_lo, re_hi, im_hi], axis=0)
        out[0, c] = (acc[c] + mm(tyi[...], rhs)).astype(out.dtype)


def inverse(grad, adj, m_hi, m_lo, pi_hi, pi_lo, tyi, bmat, used):
    slabs, chans, height, width = grad.shape
    ky = adj.shape[0] // used
    block = pl.BlockSpec((1, chans, height, width), lambda i: (i, 0, 0, 0))
    rest = (adj, m_hi, m_lo, pi_hi, pi_lo, tyi, bmat)
    return pl.pallas_call(
        functools.partial(inverse_kernel, used=used, slabs=slabs),
        grid=(slabs,),
        in_specs=[block] + [whole(t.shape) for t in rest],
        out_specs=block,
        out_shape=jax.ShapeDtypeStruct(grad.shape, grad.dtype),
        scratch_shapes=[
            pltpu.VMEM((slabs, 2, chans * ky, LANES), F32),
            pltpu.VMEM((chans, height, width), F32),
        ],
        compiler_params=params(),
        name="inverse",
        cost_estimate=pl.CostEstimate(
            flops=int(3e10), bytes_accessed=4 * grad.size, transcendentals=0
        ),
    )(grad, *rest)


def bits_of(pos, order):
    k = len(order)
    return sum(((pos >> (k - 1 - s)) & 1) << bit for s, bit in enumerate(order))


def relabel(modes, own, order):
    n = 1 << len(order)
    if n == 1:
        return modes
    per = modes.shape[0] // n
    offs = jnp.array([bits_of(p, order) for p in range(n)], jnp.int32)
    blocks = own ^ offs
    idx = (blocks[:, None] * per + jnp.arange(per, dtype=jnp.int32)[None, :]).reshape(-1)
    hit = idx[:, None] == jnp.arange(modes.shape[0], dtype=jnp.int32)[None, :]
    return jnp.sum(jnp.where(hit, modes[None, :], 0), axis=1)


def trig(phase, length):
    angles = 2.0 * math.pi / length * phase.astype(F32)
    return jnp.cos(angles), jnp.sin(angles)


def y_table(modes, length):
    pos = jnp.arange(length, dtype=jnp.int32)
    c, s = trig(modes[:, None] * pos[None, :] % length, length)
    f = 1.0 / math.sqrt(length)
    return jnp.concatenate([c, -s], axis=0) * f


def plane_tables(modes_z, modes_t, nz, nt):
    used = modes_z.shape[0] * modes_t.shape[0]
    mz = jnp.repeat(modes_z, modes_t.shape[0])
    mt = jnp.tile(modes_t, modes_z.shape[0])
    pos = jnp.arange(nz * nt, dtype=jnp.int32)
    z, t = pos // nt, pos % nt
    f = 1.0 / math.sqrt(nz * nt)
    tabs = []
    for flip in (False, True):
        if flip:
            ph = (mz[:, None] * z[None, :] % nz) * nt + (mt[:, None] * t[None, :] % nt) * nz
        else:
            ph = (z[:, None] * mz[None, :] % nz) * nt + (t[:, None] * mt[None, :] % nt) * nz
        c, s = trig(ph % (nz * nt), nz * nt)
        pad = [(0, LANES - used), (0, 0)] if flip else [(0, 0), (0, LANES - used)]
        c, s = lax.optimization_barrier((jnp.pad(c * f, pad), jnp.pad(s * f, pad)))
        if flip:
            full = jnp.concatenate(
                [jnp.concatenate([c, s], axis=1), jnp.concatenate([-s, c], axis=1)], axis=0
            )
        else:
            full = jnp.concatenate(
                [jnp.concatenate([c, -s], axis=1), jnp.concatenate([s, c], axis=1)], axis=0
            )
        tabs.append(split_table(full))
    return tabs


def x_table(modes, first, slabs, length, chans):
    pos = first + jnp.arange(slabs, dtype=jnp.int32)
    c, s = trig(pos[:, None] * modes[None, :] % length, length)
    f = 1.0 / math.sqrt(length)
    c, s = lax.optimization_barrier((c * f, s * f))
    core = jnp.stack([jnp.stack([c, -s], axis=1), jnp.stack([s, c], axis=1)], axis=0)
    eye = jnp.eye(chans, dtype=F32)
    full = core[:, :, None, :, :, None] * eye[None, None, :, None, None, :]
    kx = modes.shape[0]
    return split_table(full.reshape(2 * slabs * chans, 2 * kx * chans))


def spread_tables(chans):
    per = LANES // chans
    src = jnp.arange(LANES)
    dst = jnp.arange(chans * chans)
    grp = jnp.arange(per)
    inside = (src[None, :, None] // chans) == grp[:, None, None]
    by_c = inside & (src[None, :, None] % chans == dst[None, None, :] // chans)
    by_o = inside & (src[None, :, None] % chans == dst[None, None, :] % chans)
    twice = lambda a: jnp.concatenate([a, a], axis=1).astype(BF16)
    gather = jnp.swapaxes(by_c, 1, 2).astype(BF16)
    return twice(by_c), twice(by_o), gather


def flips(n, bit):
    return [(i, i ^ (1 << bit)) for i in range(n)]


def reduce_blocks(parts, order, n):
    data, *small = parts
    for bit in order:
        half = data.shape[0] // 2
        got = lax.ppermute(data[half:], "sp", flips(n, bit))
        data = data[:half] + got
        small = [s + lax.ppermute(s, "sp", flips(n, bit)) for s in small]
    return [data, *small]


def gather_blocks(data, order, n):
    for bit in reversed(order):
        data = jnp.concatenate([data, lax.ppermute(data, "sp", flips(n, bit))], axis=0)
    return data


def shards(
    n, field_in, out_grad, spectral_weight, bypass_weight, mode_x, mode_y, mode_z, mode_t
):
    slabs, chans, height, width = field_in.shape
    kx, ky, kz, kt = (m.shape[0] for m in (mode_x, mode_y, mode_z, mode_t))
    modes_dev = spectral_weight.shape[0]
    length = slabs * n
    own = lax.axis_index("sp").astype(jnp.int32)
    nbits = n.bit_length() - 1
    low = max(0, nbits - (ky.bit_length() - 1))
    order_y = list(range(nbits - low))
    order_z = list(range(low))
    order = [b + low for b in order_y] + order_z
    my = relabel(mode_y, own >> low, order_y)
    mz = relabel(mode_z, own & ((1 << low) - 1), order_z)
    used = kz * kt
    nt = 16
    nz = width // nt

    ty = y_table(my, height)
    ty_hi, ty_lo = split_table(ty)
    tyf = jnp.concatenate([ty_hi, ty_lo], axis=0)
    tyi = jnp.concatenate([ty_hi.T, ty_hi.T, ty_lo.T], axis=1)
    (p_hi, p_lo), (pi_hi, pi_lo) = plane_tables(mz, mode_t, nz, nt)
    m_hi, m_lo = x_table(mode_x, own * slabs, slabs, length, chans)
    by_c, by_o, summed = spread_tables(chans)
    bmat = (
        bypass_weight[:, None, :, None] * jnp.eye(16, dtype=BF16)[None, :, None, :]
    ).reshape(chans * 16, chans * 16)
    tabs = (tyf, p_hi, p_lo, m_hi, m_lo)

    part_g = forward((out_grad,), tabs, used)
    (spec_g,) = reduce_blocks([part_g], order, n)
    part_u, gram = forward((field_in, out_grad), tabs, used)
    diag = jnp.trace(gram.reshape(chans, 16, chans, 16), axis1=1, axis2=3)

    wm = spectral_weight.reshape(modes_dev, kx, kt, 2, chans * chans)
    w_re, w_im = wm[:, :, :, 0], wm[:, :, :, 1]
    adj = mix(spec_g, w_re, w_im, by_o, summed)
    spec_u, total = reduce_blocks([part_u, diag], order, n)
    adj_all = gather_blocks(adj, order, n)
    in_grad = inverse(out_grad, adj_all, m_hi, m_lo, pi_hi, pi_lo, tyi, bmat, used)
    g_re, g_im = wgrad(spec_u, spec_g, by_c, by_o, (modes_dev, kx, kt, chans * chans))
    weight_grad = jnp.stack([g_re, g_im], axis=3).reshape(modes_dev, kx * kt, 2, chans * chans)
    bypass_grad = total / math.sqrt(length * height * width)
    return (in_grad, weight_grad, bypass_grad)


def solution(mesh):
    rows = P(("grp", "sp"), None, None, None)
    return jax.shard_map(
        functools.partial(shards, mesh.shape["sp"]),
        mesh=mesh,
        in_specs=(rows, rows, P("sp", None, None, None), P(), P(), P(), P(), P()),
        out_specs=(rows, rows, P("grp", None)),
        check_vma=False,
    )
```
